32 devices in a mesh: grp: 2 (over x), wave: 16 (over z, y, core).
Axes of the slice: x: 2, y: 2, z: 4, core: 2. Of those that a mesh axis runs over, the one named last changes fastest.
Arguments:
- north_rows: bfloat16 [2560, 128, 274], P(('grp', 'wave')), parts along dimension 0, may hold values from -6 to 6
- south_rows: bfloat16 [2560, 128, 274], P(('grp', 'wave')), parts along dimension 0, may hold values from -6 to 6
- lon_counts: int32 [1280], replicated, may hold values from 20 to 5148, as said below
- slot_wave: int32 [128], replicated, may hold values from 0 to 2559, as said below
- legendre: bfloat16 [128, 1280, 1280], P('wave'), may hold values from -0.15625 to 0.15625
- mode_rates: float32 [137], replicated, may hold values from 0.05 to 20
- to_modes: bfloat16 [137, 137], replicated, may hold values from -0.5 to 0.5
- from_modes: bfloat16 [137, 137], replicated, may hold values from -0.5 to 0.5
Outputs:
- spec_state: bfloat16 [256, 1280, 274], P(('grp', 'wave')), parts along dimension 0
- new_rows: bfloat16 [2560, 128, 274], P(('grp', 'wave')), parts along dimension 0
The draws below stay inside these ranges and needn't reach their ends.
There are 2 independent parts, one for each index of `grp`. The reference program is written for one: setup_inputs(seed, part) draws one part's arguments, and reference() takes and returns one part's arrays. A program takes and returns all parts, laid end to end along the dimension named above; an argument that names none is the same for every part. Nothing has to cross between parts.
Inputs may be any that keep to these rules, and one draw needn't show every extreme that they name: Wavenumber m is present in latitude row j only if 2 m is below lon_counts[j]. `slot_wave`: distinct zonal wavenumbers.
All inputs are finite; a program needn't handle non-finite values.
Results may differ from the reference program's by a relative error of at most 0.0065.
Values may be sent and summed in bfloat16 or wider, within the bound.
A program may use at most 192 MiB of HBM per device.

```python
import math
import jax
import jax.numpy as jnp
from jax import lax

NLAT = 1280
NMAX = 2559
LEV = 137
MW = 128
NS = 1280


def draw_lon_counts(key, part):
    jitter = jax.random.randint(jax.random.fold_in(key, 11), (NLAT,), 0, 4)
    jitter = jitter.at[0].set(0).at[NLAT - 1].set(3)
    row_number = jnp.arange(NLAT, dtype=jnp.int32) + 1
    return (16 + 2 * row_number * (NMAX + 1) // NLAT + 4 * jitter).astype(jnp.int32)


def draw_slot_wave(key, part):
    inner = jax.random.permutation(jax.random.fold_in(key, 21), NMAX - 1)[:MW - 2] + 1
    values = jnp.concatenate([jnp.array([0, NMAX], dtype=jnp.int32), inner.astype(jnp.int32)])
    placing = jax.random.permutation(jax.random.fold_in(key, 22), MW)
    return values[placing].astype(jnp.int32)


def shard_levels(key, dims, split, least, top_value):
    level = 1.0
    for position, shards_of in split:
        draws = jax.random.uniform(jax.random.fold_in(jax.random.fold_in(key, 6), position), (shards_of,), jnp.float32, least / len(split), top_value / len(split))
        level = level * jnp.repeat(jnp.exp(draws), dims[position] // shards_of).reshape((-1,) + (1,) * (len(dims) - 1 - position))
    return level


def normal_values(own_key, shape, spread, most, pieces=(), kind=jnp.bfloat16):
    entries = spread * jax.random.normal(own_key, shape, jnp.float32)
    if pieces:
        entries = entries * shard_levels(own_key, shape, pieces, -0.22, 0.18)
    return jnp.clip(entries, -most, most).astype(kind)


def setup_inputs(seed: int = 0, part: int = 0) -> dict:
    arg_keys = jax.random.split(jax.random.key(seed), 9)
    part_keys = jax.random.split(jax.random.fold_in(arg_keys[8], part), 9)
    return {
        "north_rows": normal_values(part_keys[0], (NLAT, MW, 2 * LEV), 1.0, 6.0, ((0, 16),)),
        "south_rows": normal_values(part_keys[1], (NLAT, MW, 2 * LEV), 1.0, 6.0, ((0, 16),)),
        "lon_counts": draw_lon_counts(jax.random.fold_in(arg_keys[8], 71), part),
        "slot_wave": draw_slot_wave(jax.random.fold_in(arg_keys[8], 71), part),
        "legendre": normal_values(arg_keys[4], (MW, NS, NLAT), NLAT ** -0.5, 0.15625, ((0, 16),)),
        "mode_rates": jnp.clip(jnp.exp(jax.random.uniform(arg_keys[5], (LEV,), jnp.float32, math.log(0.05), math.log(20.0))), 0.05, 20.0),
        "to_modes": normal_values(arg_keys[6], (LEV, LEV), LEV ** -0.5, 0.5),
        "from_modes": normal_values(arg_keys[7], (LEV, LEV), LEV ** -0.5, 0.5),
    }


def vertical_step(direct, own_waves, mode_rates, to_modes, from_modes):
    slot_count, row_total, channels = direct.shape
    levels = to_modes.shape[0]
    modal_part = jnp.dot(direct.reshape(-1, levels), to_modes, preferred_element_type=jnp.float32)
    modal_part = modal_part.reshape(slot_count, row_total, 2, levels)
    degree = own_waves[:, None] + 2 * jnp.arange(row_total, dtype=jnp.int32)[None, :]
    degree_f = degree.astype(jnp.float32)
    scaled_degree = degree_f * (degree_f + 1.0) / float(NMAX * (NMAX + 1))
    divisor = 1.0 + mode_rates[None, None, None, :] * scaled_degree[:, :, None, None]
    scaled = (modal_part / divisor).astype(jnp.bfloat16).reshape(-1, levels)
    result = jnp.dot(scaled, from_modes, preferred_element_type=jnp.float32)
    result = result.reshape(slot_count, row_total, channels)
    return jnp.where((degree <= NMAX)[:, :, None], result, 0.0).astype(jnp.bfloat16)


def reference(north_rows, south_rows, lon_counts, slot_wave, legendre, mode_rates, to_modes, from_modes):
    live_mask = 2 * slot_wave[None, :] < lon_counts[:, None]
    summed = north_rows.astype(jnp.float32) + south_rows.astype(jnp.float32)
    symmetric = jnp.where(live_mask[:, :, None], summed, 0.0).astype(jnp.bfloat16)

    def one_slot(inputs):
        wavenumber, matrix, slot_rows, live_column = inputs
        direct = jnp.dot(matrix, slot_rows, preferred_element_type=jnp.float32).astype(jnp.bfloat16)
        state = vertical_step(direct[None], wavenumber[None], mode_rates, to_modes, from_modes)[0]
        returned = lax.dot_general(matrix, state, (((0,), (0,)), ((), ())), preferred_element_type=jnp.float32)
        returned = jnp.where(live_column[:, None], returned, 0.0).astype(jnp.bfloat16)
        return state, returned

    spec_state, returned = lax.map(one_slot, (slot_wave, legendre, jnp.moveaxis(symmetric, 1, 0), live_mask.T))
    return spec_state, jnp.moveaxis(returned, 0, 1)
```

```python
import functools

import jax
import jax.numpy as jnp
from jax import lax
from jax.experimental import pallas as pl
from jax.experimental.pallas import tpu as pltpu
from jax.sharding import PartitionSpec as P

NMAX = 2559
VMEM_LIMIT = 63 * 1024 * 1024
STEP = 16
MESH = pl.DeviceIdType.MESH


def align(rows):
    return pl.cdiv(rows, STEP) * STEP


def back_cuts(levels):
    total = 2 * levels
    ready = levels // STEP * STEP
    half = ready // 2 // STEP * STEP
    cuts = [0, half, ready]
    rest = total // STEP - ready // STEP
    for part in (1, 2):
        cuts.append(ready + rest * part // 3 * STEP)
    cuts.append(total // STEP * STEP - STEP)
    cuts.append(total)
    return tuple(zip(cuts[:-1], cuts[1:]))


def step_kernel(
    n, own, lats, levels,
    waves_s, counts_s, waves_ref, rates_ref, to_ref, from_ref, north, south, leg,
    spec_out, rows_out,
    inbuf, live, turned, sendbuf, recv, columns, returned, legbuf, to_t, from_t, rates_col,
    state_t, state_b, backbuf, backrecv, turned_back, outbuf,
    in_sem, leg_sem, send_sem, recv_sem, back_send_sem, back_recv_sem, state_sem, out_sem,
):
    me = lax.axis_index("wave")
    total = 2 * levels
    full = total // STEP
    tail = total - full * STEP
    split = align(levels)
    steps_a = split // STEP
    cuts = back_cuts(levels)

    barrier = pltpu.get_barrier_semaphore()

    def greet(r, carry):
        peer = lax.rem(me + r, n)
        pl.semaphore_signal(barrier, inc=1, device_id={"wave": peer}, device_id_type=MESH)
        return carry

    lax.fori_loop(1, n, greet, 0)

    def fetch(first, count, slot):
        return [
            pltpu.make_async_copy(
                src.at[pl.ds(first, count)],
                inbuf.at[slot, i, pl.ds(0, count)],
                in_sem.at[slot, i],
            )
            for i, src in enumerate((north, south))
        ]

    def fetch_leg(slot, place):
        return pltpu.make_async_copy(leg.at[slot], legbuf.at[place], leg_sem.at[place])

    for slot in range(2):
        for copy in fetch(slot * STEP, STEP, slot):
            copy.start()

    def fill(j, carry):
        count = counts_s[me * lats + j]
        live[pl.ds(j, 1), :] = jnp.where(2 * waves_ref[...] < count, 1.0, 0.0)
        return carry

    lax.fori_loop(0, lats, fill, 0)

    def send(src, dst, first, count, ssem, rsem):
        rows = pl.ds(first, count)

        def one(r, carry):
            peer = lax.rem(me + r, n)
            pltpu.make_async_remote_copy(
                src_ref=src.at[peer, rows],
                dst_ref=dst.at[me, rows],
                send_sem=ssem,
                recv_sem=rsem,
                device_id={"wave": peer},
                device_id_type=MESH,
            ).start()
            return carry

        lax.fori_loop(1, n, one, 0)
        pltpu.make_async_copy(src.at[me, rows], dst.at[me, rows], rsem).start()

    def pack(first, count, slot):
        sums = inbuf[slot, 0, :count].astype(jnp.float32) + inbuf[slot, 1, :count].astype(jnp.float32)
        kept = jnp.where(live[...][None] > 0.5, sums, 0.0).astype(jnp.bfloat16)
        turned[:count] = jnp.swapaxes(kept, 1, 2).astype(jnp.float32)
        for d in range(n):
            for i in range(own):
                rows = turned[:count, own * d + i, :].astype(jnp.bfloat16)
                sendbuf[d, pl.ds(first, count), lats * i : lats * (i + 1)] = rows

    def pack_step(g, carry):
        slot = lax.rem(g, 2)
        for copy in fetch(g * STEP, STEP, slot):
            copy.wait()
        pack(pl.multiple_of(g * STEP, STEP), STEP, slot)

        @pl.when(g + 2 < full)
        def _():
            for copy in fetch((g + 2) * STEP, STEP, slot):
                copy.start()

        @pl.when(g == 0)
        def _():
            pl.semaphore_wait(barrier, n - 1)

        @pl.when(g > 0)
        def _():
            part = (g - 1) // steps_a
            send(
                sendbuf, recv, pl.multiple_of((g - 1) * STEP, STEP), STEP,
                send_sem, recv_sem.at[part],
            )

        return carry

    lax.fori_loop(0, full, pack_step, 0)
    last = full * STEP - STEP
    if tail:
        for copy in fetch(full * STEP, tail, 0):
            copy.start()
        for copy in fetch(full * STEP, tail, 0):
            copy.wait()
        pack(full * STEP, tail, 0)
    for slot in range(2):
        fetch_leg(slot, slot).start()
    to_t[...] = to_ref[...].astype(jnp.float32).T.astype(jnp.bfloat16)
    from_t[...] = from_ref[...].astype(jnp.float32).T.astype(jnp.bfloat16)
    across = lax.broadcasted_iota(jnp.int32, (levels, levels), 1)
    down = lax.broadcasted_iota(jnp.int32, (levels, levels), 0)
    spread = jnp.where(across == down, jnp.broadcast_to(rates_ref[...], (levels, levels)), 0.0)
    rates_col[...] = jnp.sum(spread, axis=1, keepdims=True)
    send(sendbuf, recv, last, STEP + tail, send_sem, recv_sem.at[1])

    for part in range(2):
        arrived = recv.at[:, pl.ds(split * part, (split, total - split)[part])]
        pltpu.make_async_copy(arrived, arrived, recv_sem.at[part]).wait()
        base = levels * part
        for s in range(own):
            for d in range(n):
                piece = recv[d, base : base + levels, lats * s : lats * (s + 1)]
                columns[s, :, lats * d : lats * (d + 1)] = piece

        def solve(slot, carry):
            place = lax.rem(slot + own * part, 2)
            fetch_leg(slot, place).wait()
            wave = waves_s[me * own + slot]
            direct = lax.dot_general(
                columns[slot], legbuf[place], (((1,), (1,)), ((), ())),
                preferred_element_type=jnp.float32,
            ).astype(jnp.bfloat16)
            modal = jnp.dot(to_t[...], direct, preferred_element_type=jnp.float32)
            degree = wave + 2 * lax.broadcasted_iota(jnp.int32, (1, legbuf.shape[1]), 1)
            degree_f = degree.astype(jnp.float32)
            scaled_degree = degree_f * (degree_f + 1.0) / float(NMAX * (NMAX + 1))
            divisor = 1.0 + rates_col[...] * scaled_degree
            scaled = (modal / divisor).astype(jnp.bfloat16)
            state = jnp.dot(from_t[...], scaled, preferred_element_type=jnp.float32)
            state = jnp.where(degree <= NMAX, state, 0.0).astype(jnp.bfloat16)
            state_t[:, slot, :] = state.astype(jnp.float32)
            back = jnp.dot(state, legbuf[place], preferred_element_type=jnp.float32)
            returned[slot] = back.astype(jnp.bfloat16)
            later = slot + 2

            @pl.when(own * part + later < 2 * own)
            def _():
                fetch_leg(lax.rem(later, own), place).start()

            return carry

        lax.fori_loop(0, own, solve, 0)
        for s in range(own):
            for d in range(n):
                backbuf[d, base : base + levels, lats * s : lats * (s + 1)] = returned[
                    s, :, lats * d : lats * (d + 1)
                ]
        placed = pltpu.make_async_copy(state_b, spec_out.at[pl.ds(base, levels)], state_sem)
        if part == 1:
            pltpu.make_async_copy(state_b, spec_out.at[pl.ds(0, levels)], state_sem).wait()

        def narrow(l, carry):
            state_b[l] = state_t[l].astype(jnp.bfloat16)
            return carry

        lax.fori_loop(0, levels, narrow, 0)
        for k, (low, high) in enumerate(cuts):
            if (high <= levels) == (part == 0):
                send(backbuf, backrecv, low, high - low, back_send_sem, back_recv_sem.at[k])
        placed.start()

    def unpack(first, count, slot):
        for d in range(n):
            for i in range(own):
                rows = backrecv[d, pl.ds(first, count), lats * i : lats * (i + 1)]
                turned_back[own * d + i, :count] = rows.astype(jnp.float32)
        for c in range(count):
            flat = jnp.where(live[...] > 0.5, turned_back[:, c, :].T, 0.0)
            outbuf[slot, c] = flat.astype(jnp.bfloat16)

    def put(first, count, slot):
        return pltpu.make_async_copy(
            outbuf.at[slot, pl.ds(0, count)], rows_out.at[pl.ds(first, count)], out_sem.at[slot]
        )

    def unpack_step(g, carry):
        slot = lax.rem(g, 2)
        for k, (low, high) in enumerate(cuts):

            @pl.when(g == low // STEP)
            def _():
                landed = backrecv.at[:, pl.ds(low, high - low)]
                pltpu.make_async_copy(landed, landed, back_recv_sem.at[k]).wait()

        @pl.when(g >= 2)
        def _():
            put((g - 2) * STEP, STEP, slot).wait()

        unpack(pl.multiple_of(g * STEP, STEP), STEP, slot)
        put(g * STEP, STEP, slot).start()
        return carry

    lax.fori_loop(0, full, unpack_step, 0)
    ends = [(g * STEP, STEP, g % 2) for g in (full - 2, full - 1)]
    if tail:
        put(*ends.pop(0)).wait()
        ends.append((full * STEP, tail, full % 2))
        unpack(*ends[-1])
        put(*ends[-1]).start()
    for end in ends:
        put(*end).wait()
    placed.wait()
    sent = sendbuf.at[pl.ds(0, n - 1)]
    pltpu.make_async_copy(sent, sent, send_sem).wait()
    sent = backbuf.at[pl.ds(0, n - 1)]
    pltpu.make_async_copy(sent, sent, back_send_sem).wait()


def per_device(
    n, north_rows, south_rows, lon_counts, slot_wave, legendre, mode_rates, to_modes, from_modes
):
    lats = north_rows.shape[0]
    own, row_total, lat_total = legendre.shape
    levels = to_modes.shape[0]
    slots = slot_wave.shape[0]
    total = 2 * levels
    north = jnp.transpose(north_rows, (2, 0, 1))
    south = jnp.transpose(south_rows, (2, 0, 1))
    smem = pl.BlockSpec(memory_space=pltpu.SMEM)
    vmem = pl.BlockSpec(memory_space=pltpu.VMEM)
    hbm = pl.BlockSpec(memory_space=pl.ANY)
    bf16, f32 = jnp.bfloat16, jnp.float32
    dma = pltpu.SemaphoreType.DMA
    width = own * lats
    spec, rows = pl.pallas_call(
        functools.partial(step_kernel, n, own, lats, levels),
        in_specs=[smem, smem, vmem, vmem, vmem, vmem, hbm, hbm, hbm],
        out_specs=[hbm, hbm],
        out_shape=[
            jax.ShapeDtypeStruct((total, own, row_total), bf16),
            jax.ShapeDtypeStruct((total, lats, slots), bf16),
        ],
        scratch_shapes=[
            pltpu.VMEM((2, 2, STEP, lats, slots), bf16),
            pltpu.VMEM((lats, slots), f32),
            pltpu.VMEM((STEP, slots, lats), f32),
            pltpu.VMEM((n, total, width), bf16),
            pltpu.VMEM((n, total, width), bf16),
            pltpu.VMEM((own, levels, lat_total), bf16),
            pltpu.VMEM((own, levels, lat_total), bf16),
            pltpu.VMEM((2, row_total, lat_total), bf16),
            pltpu.VMEM((levels, levels), bf16),
            pltpu.VMEM((levels, levels), bf16),
            pltpu.VMEM((levels, 1), f32),
            pltpu.VMEM((levels, own, row_total), f32),
            pltpu.VMEM((levels, own, row_total), bf16),
            pltpu.VMEM((n, total, width), bf16),
            pltpu.VMEM((n, total, width), bf16),
            pltpu.VMEM((slots, STEP, lats), f32),
            pltpu.VMEM((2, STEP, lats, slots), bf16),
            dma((2, 2)),
            dma((2,)),
            dma,
            dma((2,)),
            dma,
            dma((len(back_cuts(levels)),)),
            dma,
            dma((2,)),
        ],
        compiler_params=pltpu.CompilerParams(
            vmem_limit_bytes=VMEM_LIMIT, collective_id=0, has_side_effects=True
        ),
        name="spectral_step",
    )(
        slot_wave, lon_counts, slot_wave[None, :], mode_rates[None, :], to_modes, from_modes,
        north, south, legendre,
    )
    return jnp.transpose(spec, (1, 2, 0)), jnp.transpose(rows, (1, 2, 0))


def solution(mesh):
    in_specs = (
        P(("grp", "wave"), None, None),
        P(("grp", "wave"), None, None),
        P(),
        P(),
        P("wave", None, None),
        P(),
        P(),
        P(),
    )
    out_specs = (P(("grp", "wave"), None, None), P(("grp", "wave"), None, None))
    body = functools.partial(per_device, mesh.shape["wave"])
    return jax.shard_map(
        body, mesh=mesh, in_specs=in_specs, out_specs=out_specs, check_vma=False
    )
```

```python
import functools

import jax
import jax.numpy as jnp
from jax import lax
from jax.experimental import pallas as pl
from jax.experimental.pallas import tpu as pltpu
from jax.sharding import PartitionSpec as P

NMAX = 2559
VMEM_LIMIT = 50 * 1024 * 1024
STEP = 16
MESH = pl.DeviceIdType.MESH


def align(rows):
    return pl.cdiv(rows, STEP) * STEP


def back_cuts(levels):
    total = 2 * levels
    ready = levels // STEP * STEP
    half = ready // 2 // STEP * STEP
    cuts = [0, half, ready]
    rest = total // STEP - ready // STEP
    for part in (1, 2):
        cuts.append(ready + rest * part // 3 * STEP)
    cuts.append(total // STEP * STEP - STEP)
    cuts.append(total)
    return tuple(zip(cuts[:-1], cuts[1:]))


def step_kernel(
    n, own, lats, levels,
    waves_s, counts_s, waves_ref, rates_ref, to_ref, from_ref, north, south, leg,
    spec_out, rows_out,
    inbuf, live, turned, sendbuf, recv, columns, legbuf, to_t, from_t, rates_col,
    state_t, backbuf, backrecv, turned_back,
    in_sem, leg_sem, send_sem, recv_sem, back_send_sem, back_recv_sem,
):
    me = lax.axis_index("wave")
    total = 2 * levels
    full = total // STEP
    tail = total - full * STEP
    split = align(levels)
    steps_a = split // STEP
    cuts = back_cuts(levels)

    barrier = pltpu.get_barrier_semaphore()

    def greet(r, carry):
        peer = lax.rem(me + r, n)
        pl.semaphore_signal(barrier, inc=1, device_id={"wave": peer}, device_id_type=MESH)
        return carry

    lax.fori_loop(1, n, greet, 0)

    def fetch(first, count, slot):
        return [
            pltpu.make_async_copy(
                src.at[pl.ds(first, count)],
                inbuf.at[slot, i, pl.ds(0, count)],
                in_sem.at[slot, i],
            )
            for i, src in enumerate((north, south))
        ]

    def fetch_leg(slot, place):
        return pltpu.make_async_copy(leg.at[slot], legbuf.at[place], leg_sem.at[place])

    for slot in range(2):
        for copy in fetch(slot * STEP, STEP, slot):
            copy.start()

    def fill(j, carry):
        count = counts_s[me * lats + j]
        live[pl.ds(j, 1), :] = jnp.where(2 * waves_ref[...] < count, 1.0, 0.0)
        return carry

    lax.fori_loop(0, lats, fill, 0)

    def send(src, dst, first, count, ssem, rsem):
        rows = pl.ds(first, count)

        def one(r, carry):
            peer = lax.rem(me + r, n)
            pltpu.make_async_remote_copy(
                src_ref=src.at[peer, rows],
                dst_ref=dst.at[me, rows],
                send_sem=ssem,
                recv_sem=rsem,
                device_id={"wave": peer},
                device_id_type=MESH,
            ).start()
            return carry

        lax.fori_loop(1, n, one, 0)
        pltpu.make_async_copy(src.at[me, rows], dst.at[me, rows], rsem).start()

    def pack(first, count, slot):
        sums = inbuf[slot, 0, :count].astype(jnp.float32) + inbuf[slot, 1, :count].astype(jnp.float32)
        kept = jnp.where(live[...][None] > 0.5, sums, 0.0).astype(jnp.bfloat16)
        turned[:count] = jnp.swapaxes(kept, 1, 2).astype(jnp.float32)
        for d in range(n):
            for i in range(own):
                rows = turned[:count, own * d + i, :].astype(jnp.bfloat16)
                sendbuf[d, pl.ds(first, count), lats * i : lats * (i + 1)] = rows

    def pack_step(g, carry):
        slot = lax.rem(g, 2)
        for copy in fetch(g * STEP, STEP, slot):
            copy.wait()
        pack(pl.multiple_of(g * STEP, STEP), STEP, slot)

        @pl.when(g + 2 < full)
        def _():
            for copy in fetch((g + 2) * STEP, STEP, slot):
                copy.start()

        @pl.when(g == 0)
        def _():
            pl.semaphore_wait(barrier, n - 1)

        @pl.when(g > 0)
        def _():
            part = (g - 1) // steps_a
            send(
                sendbuf, recv, pl.multiple_of((g - 1) * STEP, STEP), STEP,
                send_sem, recv_sem.at[part],
            )

        return carry

    lax.fori_loop(0, full, pack_step, 0)
    last = full * STEP - STEP
    if tail:
        for copy in fetch(full * STEP, tail, 0):
            copy.start()
        for copy in fetch(full * STEP, tail, 0):
            copy.wait()
        pack(full * STEP, tail, 0)
    for slot in range(2):
        fetch_leg(slot, slot).start()
    to_t[...] = to_ref[...].astype(jnp.float32).T.astype(jnp.bfloat16)
    from_t[...] = from_ref[...].astype(jnp.float32).T.astype(jnp.bfloat16)
    across = lax.broadcasted_iota(jnp.int32, (levels, levels), 1)
    down = lax.broadcasted_iota(jnp.int32, (levels, levels), 0)
    spread = jnp.where(across == down, jnp.broadcast_to(rates_ref[...], (levels, levels)), 0.0)
    rates_col[...] = jnp.sum(spread, axis=1, keepdims=True)
    send(sendbuf, recv, last, STEP + tail, send_sem, recv_sem.at[1])

    for part in range(2):
        arrived = recv.at[:, pl.ds(split * part, (split, total - split)[part])]
        pltpu.make_async_copy(arrived, arrived, recv_sem.at[part]).wait()
        base = levels * part
        for s in range(own):
            for d in range(n):
                piece = recv[d, base : base + levels, lats * s : lats * (s + 1)]
                columns[s, :, lats * d : lats * (d + 1)] = piece

        def solve(slot, carry):
            place = lax.rem(slot + own * part, 2)
            fetch_leg(slot, place).wait()
            wave = waves_s[me * own + slot]
            direct = lax.dot_general(
                columns[slot], legbuf[place], (((1,), (1,)), ((), ())),
                preferred_element_type=jnp.float32,
            ).astype(jnp.bfloat16)
            modal = jnp.dot(to_t[...], direct, preferred_element_type=jnp.float32)
            degree = wave + 2 * lax.broadcasted_iota(jnp.int32, (1, legbuf.shape[1]), 1)
            degree_f = degree.astype(jnp.float32)
            scaled_degree = degree_f * (degree_f + 1.0) / float(NMAX * (NMAX + 1))
            divisor = 1.0 + rates_col[...] * scaled_degree
            scaled = (modal / divisor).astype(jnp.bfloat16)
            state = jnp.dot(from_t[...], scaled, preferred_element_type=jnp.float32)
            state = jnp.where(degree <= NMAX, state, 0.0).astype(jnp.bfloat16)
            state_t[:, slot, :] = state.astype(jnp.float32)
            back = jnp.dot(state, legbuf[place], preferred_element_type=jnp.float32)
            columns[slot] = back.astype(jnp.bfloat16)
            later = slot + 2

            @pl.when(own * part + later < 2 * own)
            def _():
                fetch_leg(lax.rem(later, own), place).start()

            return carry

        lax.fori_loop(0, own, solve, 0)
        for s in range(own):
            for d in range(n):
                backbuf[d, base : base + levels, lats * s : lats * (s + 1)] = columns[
                    s, :, lats * d : lats * (d + 1)
                ]

        def narrow(l, carry):
            spec_out[base + l] = state_t[l].astype(jnp.bfloat16)
            return carry

        lax.fori_loop(0, levels, narrow, 0)
        for k, (low, high) in enumerate(cuts):
            if (high <= levels) == (part == 0):
                send(backbuf, backrecv, low, high - low, back_send_sem, back_recv_sem.at[k])

    def unpack(first, count):
        for d in range(n):
            for i in range(own):
                rows = backrecv[d, pl.ds(first, count), lats * i : lats * (i + 1)]
                turned_back[own * d + i, :count] = rows.astype(jnp.float32)
        for c in range(count):
            flat = jnp.where(live[...] > 0.5, turned_back[:, c, :].T, 0.0)
            rows_out[first + c] = flat.astype(jnp.bfloat16)

    def unpack_step(g, carry):
        for k, (low, high) in enumerate(cuts):

            @pl.when(g == low // STEP)
            def _():
                landed = backrecv.at[:, pl.ds(low, high - low)]
                pltpu.make_async_copy(landed, landed, back_recv_sem.at[k]).wait()

        unpack(pl.multiple_of(g * STEP, STEP), STEP)
        return carry

    lax.fori_loop(0, full, unpack_step, 0)
    if tail:
        unpack(full * STEP, tail)
    sent = sendbuf.at[pl.ds(0, n - 1)]
    pltpu.make_async_copy(sent, sent, send_sem).wait()
    sent = backbuf.at[pl.ds(0, n - 1)]
    pltpu.make_async_copy(sent, sent, back_send_sem).wait()


def per_device(
    n, north_rows, south_rows, lon_counts, slot_wave, legendre, mode_rates, to_modes, from_modes
):
    lats = north_rows.shape[0]
    own, row_total, lat_total = legendre.shape
    levels = to_modes.shape[0]
    slots = slot_wave.shape[0]
    total = 2 * levels
    north = jnp.transpose(north_rows, (2, 0, 1))
    south = jnp.transpose(south_rows, (2, 0, 1))
    smem = pl.BlockSpec(memory_space=pltpu.SMEM)
    vmem = pl.BlockSpec(memory_space=pltpu.VMEM)
    hbm = pl.BlockSpec(memory_space=pl.ANY)
    bf16, f32 = jnp.bfloat16, jnp.float32
    dma = pltpu.SemaphoreType.DMA
    width = own * lats
    spec, rows = pl.pallas_call(
        functools.partial(step_kernel, n, own, lats, levels),
        in_specs=[smem, smem, vmem, vmem, vmem, vmem, hbm, hbm, hbm],
        out_specs=[vmem, vmem],
        out_shape=[
            pltpu.VMEM((total, own, row_total), bf16),
            pltpu.VMEM((total, lats, slots), bf16),
        ],
        scratch_shapes=[
            pltpu.VMEM((2, 2, STEP, lats, slots), bf16),
            pltpu.VMEM((lats, slots), f32),
            pltpu.VMEM((STEP, slots, lats), f32),
            pltpu.VMEM((n, total, width), bf16),
            pltpu.VMEM((n, total, width), bf16),
            pltpu.VMEM((own, levels, lat_total), bf16),
            pltpu.VMEM((2, row_total, lat_total), bf16),
            pltpu.VMEM((levels, levels), bf16),
            pltpu.VMEM((levels, levels), bf16),
            pltpu.VMEM((levels, 1), f32),
            pltpu.VMEM((levels, own, row_total), f32),
            pltpu.VMEM((n, total, width), bf16),
            pltpu.VMEM((n, total, width), bf16),
            pltpu.VMEM((slots, STEP, lats), f32),
            dma((2, 2)),
            dma((2,)),
            dma,
            dma((2,)),
            dma,
            dma((len(back_cuts(levels)),)),
        ],
        compiler_params=pltpu.CompilerParams(
            vmem_limit_bytes=VMEM_LIMIT, collective_id=0, has_side_effects=True
        ),
        name="spectral_step",
    )(
        slot_wave, lon_counts, slot_wave[None, :], mode_rates[None, :], to_modes, from_modes,
        north, south, legendre,
    )
    return jnp.transpose(spec, (1, 2, 0)), jnp.transpose(rows, (1, 2, 0))


def solution(mesh):
    in_specs = (
        P(("grp", "wave"), None, None),
        P(("grp", "wave"), None, None),
        P(),
        P(),
        P("wave", None, None),
        P(),
        P(),
        P(),
    )
    out_specs = (P(("grp", "wave"), None, None), P(("grp", "wave"), None, None))
    body = functools.partial(per_device, mesh.shape["wave"])
    return jax.shard_map(
        body, mesh=mesh, in_specs=in_specs, out_specs=out_specs, check_vma=False
    )
```

```python
import functools

import jax
import jax.numpy as jnp
from jax import lax
from jax.experimental import pallas as pl
from jax.experimental.pallas import tpu as pltpu
from jax.sharding import PartitionSpec as P

NMAX = 2559
VMEM_LIMIT = 50 * 1024 * 1024
STEP = 16
MESH = pl.DeviceIdType.MESH


def align(rows):
    return pl.cdiv(rows, STEP) * STEP


def back_cuts(levels):
    total = 2 * levels
    ready = levels // STEP * STEP
    half = ready // 2 // STEP * STEP
    cuts = [0, half, ready]
    rest = total // STEP - ready // STEP
    for part in (1, 2):
        cuts.append(ready + rest * part // 3 * STEP)
    cuts.append(total // STEP * STEP - STEP)
    cuts.append(total // STEP * STEP)
    return tuple(zip(cuts[:-1], cuts[1:]))


def tail_rows(total, width):
    return max(align(total % STEP * pl.cdiv(width, 128)), STEP)


def step_kernel(
    n, own, lats, levels,
    waves_s, counts_s, waves_ref, rates_ref, to_ref, from_ref, north, south, leg,
    spec_out, rows_out,
    inbuf, live, turned, sendbuf, recv, columns, legbuf, to_t, from_t, rates_col,
    state_t, backbuf, backrecv, turned_back, tail_out, tail_in, tail_back, tail_home,
    in_sem, leg_sem, send_sem, recv_sem, back_send_sem, back_recv_sem,
    tail_send_sem, tail_recv_sem,
):
    me = lax.axis_index("wave")
    total = 2 * levels
    full = total // STEP
    tail = total - full * STEP
    split = align(levels)
    steps_a = split // STEP
    cuts = back_cuts(levels)

    barrier = pltpu.get_barrier_semaphore()

    def greet(r, carry):
        peer = lax.rem(me + r, n)
        pl.semaphore_signal(barrier, inc=1, device_id={"wave": peer}, device_id_type=MESH)
        return carry

    lax.fori_loop(1, n, greet, 0)

    def fetch(first, count, slot):
        return [
            pltpu.make_async_copy(
                src.at[pl.ds(first, count)],
                inbuf.at[slot, i, pl.ds(0, count)],
                in_sem.at[slot, i],
            )
            for i, src in enumerate((north, south))
        ]

    def fetch_leg(slot, place):
        return pltpu.make_async_copy(leg.at[slot], legbuf.at[place], leg_sem.at[place])

    for slot in range(2):
        for copy in fetch(slot * STEP, STEP, slot):
            copy.start()

    def fill(j, carry):
        count = counts_s[me * lats + j]
        live[pl.ds(j, 1), :] = jnp.where(2 * waves_ref[...] < count, 1.0, 0.0)
        return carry

    lax.fori_loop(0, lats, fill, 0)
    tail_out[...] = jnp.zeros_like(tail_out)
    tail_back[...] = jnp.zeros_like(tail_back)
    packed_rows = tail_out.shape[1]

    def send(src, dst, first, count, ssem, rsem):
        rows = pl.ds(first, count)

        def one(r, carry):
            peer = lax.rem(me + r, n)
            pltpu.make_async_remote_copy(
                src_ref=src.at[peer, rows],
                dst_ref=dst.at[me, rows],
                send_sem=ssem,
                recv_sem=rsem,
                device_id={"wave": peer},
                device_id_type=MESH,
            ).start()
            return carry

        lax.fori_loop(1, n, one, 0)
        pltpu.make_async_copy(src.at[me, rows], dst.at[me, rows], rsem).start()

    def narrow_tail(buf, packed):
        def one(d, carry):
            for t in range(pl.cdiv(own * lats, 128)):
                lanes = slice(128 * t, min(128 * (t + 1), own * lats))
                place = slice(tail * t, tail * (t + 1))
                packed[d, place, : lanes.stop - lanes.start] = buf[d, full * STEP : total, lanes]
            return carry

        lax.fori_loop(0, n, one, 0)

    def widen_tail(packed, buf, rsem):
        pltpu.make_async_copy(packed, packed, rsem).wait()

        def one(d, carry):
            for t in range(pl.cdiv(own * lats, 128)):
                lanes = slice(128 * t, min(128 * (t + 1), own * lats))
                place = slice(tail * t, tail * (t + 1))
                buf[d, full * STEP : total, lanes] = packed[d, place, : lanes.stop - lanes.start]
            return carry

        lax.fori_loop(0, n, one, 0)

    def pack(first, count, slot):
        sums = inbuf[slot, 0, :count].astype(jnp.float32) + inbuf[slot, 1, :count].astype(jnp.float32)
        kept = jnp.where(live[...][None] > 0.5, sums, 0.0).astype(jnp.bfloat16)
        turned[:count] = jnp.swapaxes(kept, 1, 2).astype(jnp.float32)
        for d in range(n):
            for i in range(own):
                rows = turned[:count, own * d + i, :].astype(jnp.bfloat16)
                sendbuf[d, pl.ds(first, count), lats * i : lats * (i + 1)] = rows

    def pack_step(g, carry):
        slot = lax.rem(g, 2)
        for copy in fetch(g * STEP, STEP, slot):
            copy.wait()
        pack(pl.multiple_of(g * STEP, STEP), STEP, slot)

        @pl.when(g + 2 < full)
        def _():
            for copy in fetch((g + 2) * STEP, STEP, slot):
                copy.start()

        @pl.when(g == 0)
        def _():
            pl.semaphore_wait(barrier, n - 1)

        @pl.when(g > 0)
        def _():
            part = (g - 1) // steps_a
            send(
                sendbuf, recv, pl.multiple_of((g - 1) * STEP, STEP), STEP,
                send_sem, recv_sem.at[part],
            )

        return carry

    lax.fori_loop(0, full, pack_step, 0)
    last = full * STEP - STEP
    if tail:
        for copy in fetch(full * STEP, tail, 0):
            copy.start()
        for copy in fetch(full * STEP, tail, 0):
            copy.wait()
        pack(full * STEP, tail, 0)
        narrow_tail(sendbuf, tail_out)
    for slot in range(2):
        fetch_leg(slot, slot).start()
    to_t[...] = to_ref[...].astype(jnp.float32).T.astype(jnp.bfloat16)
    from_t[...] = from_ref[...].astype(jnp.float32).T.astype(jnp.bfloat16)
    across = lax.broadcasted_iota(jnp.int32, (levels, levels), 1)
    down = lax.broadcasted_iota(jnp.int32, (levels, levels), 0)
    spread = jnp.where(across == down, jnp.broadcast_to(rates_ref[...], (levels, levels)), 0.0)
    rates_col[...] = jnp.sum(spread, axis=1, keepdims=True)
    send(sendbuf, recv, last, STEP, send_sem, recv_sem.at[1])
    if tail:
        send(tail_out, tail_in, 0, packed_rows, tail_send_sem.at[0], tail_recv_sem.at[0])

    def send_piece(low, high, k):
        def one_step(g, carry):
            first = pl.multiple_of(low + g * STEP, STEP)
            send(backbuf, backrecv, first, STEP, back_send_sem, back_recv_sem.at[k])
            return carry

        lax.fori_loop(0, (high - low) // STEP, one_step, 0)

    for part in range(2):
        arrived = recv.at[:, pl.ds(split * part, (split, full * STEP - split)[part])]
        pltpu.make_async_copy(arrived, arrived, recv_sem.at[part]).wait()
        if tail and part == 1:
            widen_tail(tail_in, recv, tail_recv_sem.at[0])
        base = levels * part
        for s in range(own):
            for d in range(n):
                piece = recv[d, base : base + levels, lats * s : lats * (s + 1)]
                columns[s, :, lats * d : lats * (d + 1)] = piece

        def solve(slot, carry):
            place = lax.rem(slot + own * part, 2)
            fetch_leg(slot, place).wait()
            wave = waves_s[me * own + slot]
            direct = lax.dot_general(
                columns[slot], legbuf[place], (((1,), (1,)), ((), ())),
                preferred_element_type=jnp.float32,
            ).astype(jnp.bfloat16)
            modal = jnp.dot(to_t[...], direct, preferred_element_type=jnp.float32)
            degree = wave + 2 * lax.broadcasted_iota(jnp.int32, (1, legbuf.shape[1]), 1)
            degree_f = degree.astype(jnp.float32)
            scaled_degree = degree_f * (degree_f + 1.0) / float(NMAX * (NMAX + 1))
            divisor = 1.0 + rates_col[...] * scaled_degree
            scaled = (modal / divisor).astype(jnp.bfloat16)
            state = jnp.dot(from_t[...], scaled, preferred_element_type=jnp.float32)
            state = jnp.where(degree <= NMAX, state, 0.0).astype(jnp.bfloat16)
            state_t[:, slot, :] = state.astype(jnp.float32)
            back = jnp.dot(state, legbuf[place], preferred_element_type=jnp.float32)
            columns[slot] = back.astype(jnp.bfloat16)
            later = slot + 2

            @pl.when(own * part + later < 2 * own)
            def _():
                fetch_leg(lax.rem(later, own), place).start()

            return carry

        lax.fori_loop(0, own, solve, 0)
        for s in range(own):
            for d in range(n):
                backbuf[d, base : base + levels, lats * s : lats * (s + 1)] = columns[
                    s, :, lats * d : lats * (d + 1)
                ]

        if tail and part == 1:
            narrow_tail(backbuf, tail_back)

        def narrow(l, carry):
            spec_out[base + l] = state_t[l].astype(jnp.bfloat16)
            return carry

        lax.fori_loop(0, levels, narrow, 0)
        for k, (low, high) in enumerate(cuts):
            if (high <= levels) == (part == 0):
                send_piece(low, high, k)
        if tail and part == 1:
            send(tail_back, tail_home, 0, packed_rows, tail_send_sem.at[1], tail_recv_sem.at[1])

    def unpack(first, count):
        for d in range(n):
            for i in range(own):
                rows = backrecv[d, pl.ds(first, count), lats * i : lats * (i + 1)]
                turned_back[own * d + i, :count] = rows.astype(jnp.float32)
        for c in range(count):
            flat = jnp.where(live[...] > 0.5, turned_back[:, c, :].T, 0.0)
            rows_out[first + c] = flat.astype(jnp.bfloat16)

    def unpack_step(g, carry):
        for k, (low, high) in enumerate(cuts):

            @pl.when(g == low // STEP)
            def _():
                landed = backrecv.at[:, pl.ds(low, high - low)]
                pltpu.make_async_copy(landed, landed, back_recv_sem.at[k]).wait()

        unpack(pl.multiple_of(g * STEP, STEP), STEP)
        return carry

    lax.fori_loop(0, full, unpack_step, 0)
    if tail:
        widen_tail(tail_home, backrecv, tail_recv_sem.at[1])
        unpack(full * STEP, tail)
        for k, buf in enumerate((tail_out, tail_back)):
            sent = buf.at[pl.ds(0, n - 1)]
            pltpu.make_async_copy(sent, sent, tail_send_sem.at[k]).wait()
    sent = sendbuf.at[pl.ds(0, n - 1), pl.ds(0, full * STEP)]
    pltpu.make_async_copy(sent, sent, send_sem).wait()
    sent = backbuf.at[pl.ds(0, n - 1), pl.ds(0, full * STEP)]
    pltpu.make_async_copy(sent, sent, back_send_sem).wait()


def per_device(
    n, north_rows, south_rows, lon_counts, slot_wave, legendre, mode_rates, to_modes, from_modes
):
    lats = north_rows.shape[0]
    own, row_total, lat_total = legendre.shape
    levels = to_modes.shape[0]
    slots = slot_wave.shape[0]
    total = 2 * levels
    north = jnp.transpose(north_rows, (2, 0, 1))
    south = jnp.transpose(south_rows, (2, 0, 1))
    smem = pl.BlockSpec(memory_space=pltpu.SMEM)
    vmem = pl.BlockSpec(memory_space=pltpu.VMEM)
    hbm = pl.BlockSpec(memory_space=pl.ANY)
    bf16, f32 = jnp.bfloat16, jnp.float32
    dma = pltpu.SemaphoreType.DMA
    width = own * lats
    spec, rows = pl.pallas_call(
        functools.partial(step_kernel, n, own, lats, levels),
        in_specs=[smem, smem, vmem, vmem, vmem, vmem, hbm, hbm, hbm],
        out_specs=[vmem, vmem],
        out_shape=[
            pltpu.VMEM((total, own, row_total), bf16),
            pltpu.VMEM((total, lats, slots), bf16),
        ],
        scratch_shapes=[
            pltpu.VMEM((2, 2, STEP, lats, slots), bf16),
            pltpu.VMEM((lats, slots), f32),
            pltpu.VMEM((STEP, slots, lats), f32),
            pltpu.VMEM((n, total, width), bf16),
            pltpu.VMEM((n, total, width), bf16),
            pltpu.VMEM((own, levels, lat_total), bf16),
            pltpu.VMEM((2, row_total, lat_total), bf16),
            pltpu.VMEM((levels, levels), bf16),
            pltpu.VMEM((levels, levels), bf16),
            pltpu.VMEM((levels, 1), f32),
            pltpu.VMEM((levels, own, row_total), f32),
            pltpu.VMEM((n, total, width), bf16),
            pltpu.VMEM((n, total, width), bf16),
            pltpu.VMEM((slots, STEP, lats), f32),
            *[pltpu.VMEM((n, tail_rows(total, width), 128), bf16)] * 4,
            dma((2, 2)),
            dma((2,)),
            dma,
            dma((2,)),
            dma,
            dma((len(back_cuts(levels)),)),
            dma((2,)),
            dma((2,)),
        ],
        compiler_params=pltpu.CompilerParams(
            vmem_limit_bytes=VMEM_LIMIT, collective_id=0, has_side_effects=True
        ),
        name="spectral_step",
    )(
        slot_wave, lon_counts, slot_wave[None, :], mode_rates[None, :], to_modes, from_modes,
        north, south, legendre,
    )
    return jnp.transpose(spec, (1, 2, 0)), jnp.transpose(rows, (1, 2, 0))


def solution(mesh):
    in_specs = (
        P(("grp", "wave"), None, None),
        P(("grp", "wave"), None, None),
        P(),
        P(),
        P("wave", None, None),
        P(),
        P(),
        P(),
    )
    out_specs = (P(("grp", "wave"), None, None), P(("grp", "wave"), None, None))
    body = functools.partial(per_device, mesh.shape["wave"])
    return jax.shard_map(
        body, mesh=mesh, in_specs=in_specs, out_specs=out_specs, check_vma=False
    )
```
